1024 devices in a mesh: ga: 64 (over x_lo, z, core), gp: 16 (over y, x_hi).
Axes of the slice: x: 8 (x_hi: 2, x_lo: 4; x = x_hi * 4 + x_lo), y: 8, z: 8, core: 2. Of those that a mesh axis runs over, the one named last changes fastest.
Arguments:
- matel: bfloat16 [128, 16, 100352], P('ga', None, 'gp'), may hold values from -0.01953125 to 0.01953125
- pole_amp: bfloat16 [8192, 100352], P('ga', 'gp'), may hold values from -6 to 6
- pole_freq: bfloat16 [8192, 100352], P('ga', 'gp'), may hold values from 0.5 to 4
- band_energy: float32 [128], replicated, may hold values from -3 to 3
- energies: float32 [3], replicated, may hold values from -2 to 2
- owner: int32 [5], replicated, may hold values from 0 to 63
- slot: int32 [5], replicated, may hold values from 0 to 1
Outputs:
- sigma: float32 [3, 16, 16], replicated
The draws below stay inside these ranges and needn't reach their ends.
Inputs may be any that keep to these rules, and one draw needn't show every extreme that they name: `slot`: position among the 2 bands stored by that row.
All inputs are finite; a program needn't handle non-finite values.
Results may differ from the reference program's by a relative error of at most 0.0029.
Values may be sent and summed in bfloat16 or wider, within the bound.
A program may use at most 128 MiB of HBM per device.

```python
import math
import jax
import jax.numpy as jnp
from jax import lax

NG = 100352
TG = 128
NS = 16
HOLD = 2
WIN = 5
NE = 3
RG = 8192
BANDS = 128
N_GA = 64


def touch_ends(values, stream_key, least, largest):
    spot = [jax.random.randint(jax.random.fold_in(stream_key, axis), (), 0, length) for axis, length in enumerate(values.shape)]
    widest = values.shape.index(max(values.shape))
    next_to = spot[:widest] + [(spot[widest] + 1) % values.shape[widest]] + spot[widest + 1:]
    return values.at[tuple(spot)].set(least).at[tuple(next_to)].set(largest)


def block_scale(key, extent, split, low, high):
    def one(position, blocks):
        draws = jax.random.uniform(jax.random.fold_in(jax.random.fold_in(key, 6), position), (blocks,), jnp.float32, low / len(split), high / len(split))
        return jnp.repeat(jnp.exp(draws), extent[position] // blocks).reshape((-1,) + (1,) * (len(extent) - position - 1))

    level = one(*split[0])
    for cut in split[1:]:
        level = level * one(*cut)
    return level


def centred(stream_key, extent, width, reach, pieces=(), held_as=jnp.bfloat16):
    loudness = block_scale(stream_key, extent, pieces, -0.22, 0.18) if pieces else 1.0
    values = jax.random.normal(stream_key, extent, jnp.float32) * width * loudness
    return jnp.minimum(jnp.maximum(values, -reach), reach).astype(held_as)


def setup_inputs(seed: int = 0) -> dict:
    key_list = jax.random.split(jax.random.key(seed), 8)
    return {
        "matel": centred(key_list[0], (BANDS, NS, NG), NG ** -0.5, 0.01953125, ((0, 64), (2, 16))),
        "pole_amp": centred(key_list[1], (RG, NG), 1.0, 6.0, ((0, 64), (1, 16))),
        "pole_freq": jnp.clip(jnp.exp(math.log(4.0) - 2.0794415 * jax.random.uniform(key_list[2], (RG, NG), jnp.float32) ** block_scale(key_list[2], (RG, NG), ((0, 64), (1, 16)), -0.2, 0.2)), 0.5, 4.0).astype(jnp.bfloat16),
        "band_energy": jnp.clip(jax.random.uniform(key_list[3], (BANDS,), jnp.float32, -3.0, 3.0), -3.0, 3.0),
        "energies": jnp.clip(jax.random.uniform(key_list[4], (NE,), jnp.float32, -2.0, 2.0), -2.0, 2.0),
        "owner": touch_ends(jax.random.randint(key_list[5], (WIN,), 0, N_GA), jax.random.fold_in(key_list[5], 1), 0, N_GA - 1).astype(jnp.int32),
        "slot": touch_ends(jax.random.randint(key_list[6], (WIN,), 0, HOLD), jax.random.fold_in(key_list[6], 1), 0, HOLD - 1).astype(jnp.int32),
    }


def reference(matel, pole_amp, pole_freq, band_energy, energies, owner, slot):
    band_index = (owner * HOLD + slot).astype(jnp.int32)
    chosen = matel[band_index]
    levels = band_energy[band_index]
    amp_blocks = pole_amp.reshape(N_GA, TG, NG)
    freq_blocks = pole_freq.reshape(N_GA, TG, NG)
    starts = jnp.arange(N_GA, dtype=jnp.int32) * TG

    def add_block(partial_value, inputs):
        amplitude_block, frequency_block, row_start = inputs
        amplitude = amplitude_block.astype(jnp.float32)
        frequency = frequency_block.astype(jnp.float32)
        numerator = amplitude * frequency
        squared = frequency * frequency
        row_pieces = lax.dynamic_slice_in_dim(chosen, row_start.astype(jnp.int32), TG, 2)
        for band_slot in range(WIN):
            detuning = energies[:, None, None] - levels[band_slot]
            pole_value = (numerator / (detuning * detuning + squared)).astype(jnp.bfloat16)
            pole_value = lax.optimization_barrier(pole_value)
            folded = jnp.einsum("egk,sk->esg", pole_value.astype(jnp.float32), chosen[band_slot].astype(jnp.float32))
            partial_value = partial_value + jnp.einsum("tg,esg->ets", row_pieces[band_slot].astype(jnp.float32), folded, precision=lax.Precision.HIGHEST)
        return partial_value, None

    initial = jnp.zeros((NE, NS, NS), jnp.float32)
    sigma_sum, unused = lax.scan(add_block, initial, (amp_blocks, freq_blocks, starts))
    return sigma_sum
```

```python
import functools

import jax
import jax.numpy as jnp
from jax import lax
from jax.experimental import pallas as pl
from jax.experimental.pallas import tpu as pltpu
from jax.sharding import PartitionSpec as P

MESH = pl.DeviceIdType.MESH
NX, NY, NZ = 8, 8, 8
XLO = 4
LANES = 128
BANDS = 5
ENERGIES = 3
STATES = 16
ROWS = 128
TILES = 49
POSITIONS = 64
HALF = POSITIONS // 2


def place(position):
    x, z, core = lax.div(position, 16), lax.rem(lax.div(position, 2), NZ), lax.rem(position, 2)
    return core, jnp.where(core == 0, x * NZ + z, z * XLO + x)


def kernel(
    owner, slot, band_energy, energies, matel, amp, freq, out,
    held, amp_v, freq_v, masked, from_core, merged, from_first, summed, from_second, final,
    columns, joined, pole, rows, share, totals,
    load_sem, core_send, core_recv, first_send, first_recv, second_send, second_recv,
    spread_send, spread_recv, wide_send, wide_recv, pair_send, pair_recv,
    rows_send, rows_recv, sigma_send, sigma_recv,
):
    ga, gp = lax.axis_index("ga"), lax.axis_index("gp")
    x_lo, z, core = lax.div(ga, 16), lax.rem(lax.div(ga, 2), NZ), lax.rem(ga, 2)
    y, x_hi = lax.div(gp, 2), lax.rem(gp, 2)
    x = x_hi * XLO + x_lo

    def device(x_at, y_at, z_at, core_at):
        return (
            lax.rem(x_at, XLO) * 16 + z_at * 2 + core_at,
            y_at * 2 + lax.div(x_at, XLO),
        )

    other_core = device(x, y, z, 1 - core)

    def along_x(d):
        return device(lax.rem(x + d, NX), y, z, core)

    def along_y(d):
        return device(x, lax.rem(y + d, NY), z, core)

    def along_z(d):
        return device(x, y, lax.rem(z + d, NZ), core)

    def within_x(d):
        return device(x_hi * XLO + lax.rem(x_lo + d, XLO), y, z, core)

    load_matel = pltpu.make_async_copy(matel, held, load_sem.at[0])
    load_amp = pltpu.make_async_copy(amp, amp_v, load_sem.at[1])
    load_freq = pltpu.make_async_copy(freq, freq_v, load_sem.at[2])
    load_matel.start()
    load_amp.start()
    load_freq.start()

    barrier = pltpu.get_barrier_semaphore()
    pl.semaphore_signal(barrier, inc=1, device_id=other_core, device_id_type=MESH)
    for peer in (along_x, along_y, along_z):
        for d in range(1, 8):
            pl.semaphore_signal(barrier, inc=1, device_id=peer(d), device_id_type=MESH)

    shift = jnp.where(gp == 1, TILES, 0)
    own = [owner[k] == ga for k in range(BANDS)]
    pick = [slot[k] for k in range(BANDS)]
    squares = []
    for k in range(BANDS):
        level = band_energy[owner[k] * 2 + slot[k]]
        for e in range(ENERGIES):
            detuning = energies[e] - level
            squares.append(detuning * detuning)

    with jax.named_scope('load'):
        load_matel.wait()

    def mask_one(position, carry):
        tile = jnp.minimum(lax.rem(position + POSITIONS - shift, POSITIONS), TILES - 1)
        lanes = pl.ds(pl.multiple_of(tile * LANES, LANES), LANES)
        side, index = place(position)
        for k in range(BANDS):
            value = held[pick[k], :, lanes]
            masked[side, k, index] = jnp.where(own[k], value, jnp.zeros_like(value))
        return carry

    with jax.named_scope('mask'):
        lax.fori_loop(0, POSITIONS, mask_one, 0)

    with jax.named_scope('barrier'):
        pl.semaphore_wait(barrier, 22)

    def send(src, dst, send_sem, recv_sem, to):
        pltpu.make_async_remote_copy(
            src_ref=src, dst_ref=dst, send_sem=send_sem, recv_sem=recv_sem,
            device_id=to, device_id_type=MESH,
        ).start()

    def wait(ref, sem):
        pltpu.make_async_copy(ref, ref, sem).wait()

    for k in range(BANDS):
        send(masked.at[1 - core, k], from_core.at[k], core_send.at[k], core_recv.at[k], other_core)

    load_amp.wait()
    load_freq.wait()

    def pole_tiles(first, last):
        def one(tile, carry):
            lanes = pl.ds(pl.multiple_of(tile * LANES, LANES), LANES)
            for r in range(0, ROWS, 16):
                amplitude = amp_v[r : r + 16, lanes].astype(jnp.float32)
                frequency = freq_v[r : r + 16, lanes].astype(jnp.float32)
                numerator = amplitude * frequency
                squared = frequency * frequency
                for k in range(BANDS):
                    for e in range(ENERGIES):
                        value = numerator / (squares[k * ENERGIES + e] + squared)
                        pole[k, e * ROWS + r : e * ROWS + r + 16, lanes] = value.astype(jnp.bfloat16)
            return carry

        lax.fori_loop(first, last, one, 0)

    with jax.named_scope('pole'):
        pole_tiles(0, 8)

    def per_core(body):
        @pl.when(core == 0)
        def _():
            body(XLO, NZ, x_lo, z, within_x, along_z)

        @pl.when(core == 1)
        def _():
            body(NZ, XLO, z, x_lo, along_z, within_x)

    def loop(body):
        def step(k, carry):
            body(k)
            return carry

        lax.fori_loop(0, BANDS, step, 0)

    def to_first(n1, n2, me1, me2, peer1, peer2):
        def band(k):
            wait(from_core.at[k], core_recv.at[k])
            merged[k] = masked[core, k] + from_core[k]
            for d in range(1, n1):
                target = lax.rem(me1 + d, n1)
                send(
                    merged.at[k, pl.ds(target * n2, n2)],
                    from_first.at[k, pl.ds((d - 1) * n2, n2)],
                    first_send.at[k], first_recv.at[k], peer1(d),
                )

        loop(band)

    with jax.named_scope('to_first'):
        per_core(to_first)
    with jax.named_scope('pole'):
        pole_tiles(8, 30)

    def to_second(n1, n2, me1, me2, peer1, peer2):
        def band(k):
            wait(from_first.at[k, pl.ds(0, (n1 - 1) * n2)], first_recv.at[k])
            total = merged[k, pl.ds(me1 * n2, n2)]
            for d in range(1, n1):
                total = total + from_first[k, pl.ds((d - 1) * n2, n2)]
            summed[k, pl.ds(0, n2)] = total
            for d in range(1, n2):
                send(
                    summed.at[k, lax.rem(me2 + d, n2)], from_second.at[k, d - 1],
                    second_send.at[k], second_recv.at[k], peer2(d),
                )

        loop(band)

    with jax.named_scope('to_second'):
        per_core(to_second)
    with jax.named_scope('pole'):
        pole_tiles(30, TILES)

    def spread(n1, n2, me1, me2, peer1, peer2):
        def band(k):
            wait(from_second.at[k, pl.ds(0, n2 - 1)], second_recv.at[k])
            total = summed[k, me2]
            for d in range(1, n2):
                total = total + from_second[k, d - 1]
            final[k] = total
            index = me1 * n2 + me2
            columns[core, k, index] = total
            for d in range(1, n2):
                send(final.at[k], columns.at[core, k, index], spread_send.at[k], spread_recv.at[k], peer2(d))

        loop(band)

    with jax.named_scope('spread'):
        per_core(spread)

    source = ((gp == 0) & (ga < TILES)) | ((gp == 1) & (ga >= TILES))
    relay = (y == 0) & jnp.logical_not(source)

    @pl.when(source)
    def _():
        send(final, rows, rows_send.at[0], rows_recv.at[0], along_x(XLO))
        for k in range(BANDS):
            rows[k] = final[k]

    def widen(n1, n2, me1, me2, peer1, peer2):
        def band(k):
            wait(from_second.at[k, pl.ds(0, n2 - 1)], spread_recv.at[k])
            piece = columns.at[core, k, pl.ds(me1 * n2, n2)]
            for d in range(1, n1):
                send(piece, piece, wide_send.at[k], wide_recv.at[k], peer1(d))

        loop(band)

    with jax.named_scope('widen'):
        per_core(widen)

    @pl.when(relay)
    def _():
        with jax.named_scope('relay'):
            wait(rows, rows_recv.at[0])

    @pl.when(y == 0)
    def _():
        for d in range(1, NY):
            send(rows, rows, rows_send.at[1], rows_recv.at[1], along_y(d))

    def fold(k):
        with jax.named_scope('pair'):
            wait(columns.at[1 - core, k], pair_recv.at[k])

        def join(tile, carry):
            side, index = place(lax.rem(tile + shift, POSITIONS))
            joined[:, pl.ds(pl.multiple_of(tile * LANES, LANES), LANES)] = columns[side, k, index]
            return carry

        lax.fori_loop(0, TILES, join, 0)
        folded = lax.dot_general(
            pole[k], joined[...], (((1,), (1,)), ((), ())), preferred_element_type=jnp.float32
        )
        return jnp.concatenate([folded[e * ROWS : (e + 1) * ROWS] for e in range(ENERGIES)], axis=1)

    def contract(k, folded):
        share[:, 0 : ENERGIES * STATES] += jnp.dot(
            rows[k].astype(jnp.float32), folded,
            precision=lax.Precision.HIGHEST, preferred_element_type=jnp.float32,
        )

    share[...] = jnp.zeros_like(share)

    def forward(k):
        def pieces(n1, n2, me1, me2, peer1, peer2):
            wait(from_first.at[k, pl.ds(0, (n1 - 1) * n2)], wide_recv.at[k])

        per_core(pieces)
        send(columns.at[core, k], columns.at[core, k], pair_send.at[k], pair_recv.at[k], other_core)

    with jax.named_scope('forward'):
        forward(0)

    @pl.when(y > 0)
    def _():
        with jax.named_scope('rows'):
            wait(rows, rows_recv.at[1])

    def advance(k, carry):
        @pl.when(k < BANDS)
        def _():
            with jax.named_scope('forward'):
                forward(k)

        with jax.named_scope('fold'):
            folded = fold(k - 1)
        with jax.named_scope('contract'):
            contract(k - 1, folded)
        return carry

    lax.fori_loop(1, BANDS + 1, advance, 0)

    packed = jnp.concatenate([share[0:8, 0:64], share[8:16, 0:64]], axis=1)
    stages = ((2, core, None), (NX, x, along_x), (NY, y, along_y), (NZ, z, along_z))
    for stage, (n, me, peer) in enumerate(stages):
        totals[stage, me] = packed
        mine = totals.at[stage, me]
        for d in range(1, n):
            send(mine, mine, sigma_send.at[stage], sigma_recv.at[stage], other_core if peer is None else peer(d))
        with jax.named_scope('sigma'):
            wait(totals.at[stage, pl.ds(0, n - 1)], sigma_recv.at[stage])
        packed = totals[stage, 0]
        for d in range(1, n):
            packed = packed + totals[stage, d]

    for e in range(ENERGIES):
        out[e, 0:8] = packed[:, e * STATES : (e + 1) * STATES]
        out[e, 8:16] = packed[:, 64 + e * STATES : 64 + (e + 1) * STATES]

    def drain(n1, n2, me1, me2, peer1, peer2):
        def band(k):
            wait(from_core.at[k], core_send.at[k])
            wait(from_first.at[k, pl.ds(0, (n1 - 1) * n2)], first_send.at[k])
            wait(from_second.at[k, pl.ds(0, n2 - 1)], second_send.at[k])
            wait(from_second.at[k, pl.ds(0, n2 - 1)], spread_send.at[k])
            wait(from_first.at[k, pl.ds(0, (n1 - 1) * n2)], wide_send.at[k])
            wait(from_core.at[k], pair_send.at[k])

        loop(band)

    with jax.named_scope('drain'):
        per_core(drain)

    @pl.when(source)
    def _():
        wait(rows, rows_send.at[0])

    @pl.when(y == 0)
    def _():
        wait(from_second, rows_send.at[1])

    for stage, n in enumerate((2, NX, NY, NZ)):
        wait(totals.at[stage, pl.ds(0, n - 1)], sigma_send.at[stage])


def shards(matel, pole_amp, pole_freq, band_energy, energies, owner, slot):
    bf16, f32 = jnp.bfloat16, jnp.float32
    dma = pltpu.SemaphoreType.DMA
    cols = matel.shape[2]
    return pl.pallas_call(
        kernel,
        out_shape=jax.ShapeDtypeStruct((ENERGIES, STATES, STATES), f32),
        in_specs=[pl.BlockSpec(memory_space=pltpu.SMEM)] * 4 + [pl.BlockSpec(memory_space=pl.ANY)] * 3,
        out_specs=pl.BlockSpec(memory_space=pltpu.VMEM),
        scratch_shapes=[
            pltpu.VMEM(matel.shape, bf16),
            pltpu.VMEM((ROWS, cols), bf16),
            pltpu.VMEM((ROWS, cols), bf16),
            pltpu.VMEM((2, BANDS, HALF, STATES, LANES), bf16),
            pltpu.VMEM((BANDS, HALF, STATES, LANES), bf16),
            pltpu.VMEM((BANDS, HALF, STATES, LANES), bf16),
            pltpu.VMEM((BANDS, 28, STATES, LANES), bf16),
            pltpu.VMEM((BANDS, 8, STATES, LANES), bf16),
            pltpu.VMEM((BANDS, 7, STATES, LANES), bf16),
            pltpu.VMEM((BANDS, STATES, LANES), bf16),
            pltpu.VMEM((2, BANDS, HALF, STATES, LANES), bf16),
            pltpu.VMEM((STATES, cols), bf16),
            pltpu.VMEM((BANDS, ENERGIES * ROWS, cols), bf16),
            pltpu.VMEM((BANDS, STATES, LANES), bf16),
            pltpu.VMEM((STATES, LANES), f32),
            pltpu.VMEM((4, 8, 8, LANES), f32),
            dma((3,)),
        ] + [dma((BANDS,))] * 12 + [dma((2,)), dma((2,)), dma((4,)), dma((4,))],
        compiler_params=pltpu.CompilerParams(
            collective_id=0, has_side_effects=True, vmem_limit_bytes=60 * 1024 * 1024
        ),
    )(owner, slot, band_energy, energies, matel, pole_amp, pole_freq)


def solution(mesh):
    return jax.shard_map(
        shards,
        mesh=mesh,
        in_specs=(P("ga", None, "gp"), P("ga", "gp"), P("ga", "gp"), P(), P(), P(), P()),
        out_specs=P(),
        check_vma=False,
    )
```

```python
import jax
import jax.numpy as jnp
from jax import lax
from jax.experimental import pallas as pl
from jax.experimental.pallas import tpu as pltpu
from jax.sharding import PartitionSpec as P

MESH = pl.DeviceIdType.MESH
NX, NY, NZ = 8, 8, 8
XLO = 4
LANES = 128
BANDS = 5
ENERGIES = 3
STATES = 16
ROWS = 128
TILES = 49
WIDE0, WIDE1 = 7 * LANES, 3 * LANES
START1 = 28 * LANES
COLS = TILES * LANES


def kernel(
    owner_in, slot_in, band_energy_in, energies_in, matel, amp, freq, out,
    owner, slot, band_energy, energies,
    amp_v, freq_v, near0, near1, chosen0, chosen1, far, final, columns, pole, rows, folded, share, totals, totals_z,
    load_sem, small_sem, first_send, first_recv, second_send, second_recv, spread_send, spread_recv,
    wide_send, wide_recv, pair_send, pair_recv, rows_send, rows_recv, sigma_send, sigma_recv,
):
    ga, gp = lax.axis_index("ga"), lax.axis_index("gp")
    x_lo, z, core = lax.div(ga, 16), lax.rem(lax.div(ga, 2), NZ), lax.rem(ga, 2)
    y, x_hi = lax.div(gp, 2), lax.rem(gp, 2)
    x = x_hi * XLO + x_lo

    def device(x_at, y_at, z_at, core_at):
        return (
            lax.rem(x_at, XLO) * 16 + z_at * 2 + core_at,
            y_at * 2 + lax.div(x_at, XLO),
        )

    def near(x_lo_at, z_at, core_at):
        return (x_lo_at * 16 + z_at * 2 + core_at, gp)

    def along_x(d):
        return device(lax.rem(x + d, NX), y, z, core)

    def along_y(d):
        return device(x, lax.rem(y + d, NY), z, core)

    def along_z(d):
        return near(x_lo, lax.rem(z + d, NZ), core)

    def within_x(d):
        return near(lax.rem(x_lo + d, XLO), z, core)

    other_core = near(x_lo, z, 1 - core)

    def send(src, dst, send_sem, recv_sem, to):
        pltpu.make_async_remote_copy(
            src_ref=src, dst_ref=dst, send_sem=send_sem, recv_sem=recv_sem,
            device_id=to, device_id_type=MESH,
        ).start()

    def wait(ref, sem):
        pltpu.make_async_copy(ref, ref, sem).wait()

    small = [
        pltpu.make_async_copy(src, dst, small_sem.at[i])
        for i, (src, dst) in enumerate(
            ((owner_in, owner), (slot_in, slot), (band_energy_in, band_energy), (energies_in, energies))
        )
    ]
    for copy in small:
        copy.start()
    load_amp = pltpu.make_async_copy(amp, amp_v, load_sem.at[1])
    load_freq = pltpu.make_async_copy(freq, freq_v, load_sem.at[2])

    tile = jnp.where(core == 0, x_lo * 7 + z, 28 + z * 3 + x_lo)
    collects = (z < 7) & ((core == 0) | (x_lo < 3))
    source = (y == 0) & collects & ((x_hi == 0) | (tile < 15))
    target = tile + jnp.where(x_hi == 0, 0, TILES)
    own_target = source & (target == ga)
    wanted = jnp.where(ga < TILES, ga, ga - TILES)
    wanted_hi = jnp.where(ga < TILES, 0, 1)
    second_set = jnp.maximum(wanted - 28, 0)
    collector = jnp.where(
        wanted < 28,
        lax.div(wanted, 7) * 16 + lax.rem(wanted, 7) * 2,
        lax.rem(second_set, 3) * 16 + lax.div(second_set, 3) * 2 + 1,
    )
    own_collector = (collector == ga) & (x_hi == wanted_hi)

    barrier = pltpu.get_barrier_semaphore()

    def signal(to):
        pl.semaphore_signal(barrier, inc=1, device_id=to, device_id_type=MESH)

    signal(other_core)
    for d in range(1, 8):
        signal(along_z(d))
        signal(near(x_lo, lax.rem(z + d, NZ), 1 - core))
        signal(along_x(d))
        signal(along_y(d))
    for d in range(1, XLO):
        signal(near(lax.rem(x_lo + d, XLO), z, 1 - core))

    @pl.when((y == 0) & jnp.logical_not(own_collector))
    def _():
        signal((collector, wanted_hi))

    load_amp.start()
    load_freq.start()
    extra = jnp.where(source, 2, 0) - jnp.where(own_target, 1, 0)
    with jax.named_scope("barrier"):
        pl.semaphore_wait(barrier, 32 + extra)

    own0 = pltpu.make_async_copy(
        matel.at[:, :, pl.ds(x_lo * WIDE0, WIDE0)], near0.at[x_lo * 2], load_sem.at[0]
    )
    own1 = pltpu.make_async_copy(
        matel.at[:, :, pl.ds(START1 + lax.rem(z, 7) * WIDE1, WIDE1)], near1.at[z * 2 + 1], load_sem.at[0]
    )
    for d in range(1, XLO):
        to = lax.rem(x_lo + d, XLO)
        send(
            matel.at[:, :, pl.ds(to * WIDE0, WIDE0)], near0.at[x_lo * 2 + core],
            first_send.at[0], first_recv, near(to, z, 0),
        )
    for d in range(1, NZ):
        to = lax.rem(z + d, NZ)

        @pl.when(to < 7)
        def _():
            send(
                matel.at[:, :, pl.ds(START1 + lax.rem(to, 7) * WIDE1, WIDE1)], near1.at[z * 2 + core],
                first_send.at[1], first_recv, near(x_lo, to, 1),
            )

    @pl.when(core == 0)
    def _():
        own0.start()

        @pl.when(z < 7)
        def _():
            send(
                matel.at[:, :, pl.ds(START1 + lax.rem(z, 7) * WIDE1, WIDE1)], near1.at[z * 2],
                first_send.at[2], first_recv, other_core,
            )

    @pl.when(core == 1)
    def _():
        send(
            matel.at[:, :, pl.ds(x_lo * WIDE0, WIDE0)], near0.at[x_lo * 2 + 1],
            first_send.at[2], first_recv, other_core,
        )

        @pl.when(z < 7)
        def _():
            own1.start()

    for copy in small:
        copy.wait()
    pick, owner_x, owner_z, owner_core, squares = [], [], [], [], []
    for k in range(BANDS):
        row = owner[k]
        pick.append(slot[k])
        owner_x.append(lax.div(row, 16))
        owner_z.append(lax.rem(lax.div(row, 2), NZ))
        owner_core.append(lax.rem(row, 2))
        level = band_energy[row * 2 + slot[k]]
        for e in range(ENERGIES):
            detuning = energies[e] - level
            squares.append(detuning * detuning)

    load_amp.wait()
    load_freq.wait()

    def pole_tiles(first, last):
        def one(at, carry):
            lanes = pl.ds(pl.multiple_of(at * LANES, LANES), LANES)
            for r in range(0, ROWS, 16):
                amplitude = amp_v[r : r + 16, lanes].astype(jnp.float32)
                frequency = freq_v[r : r + 16, lanes].astype(jnp.float32)
                numerator = amplitude * frequency
                squared = frequency * frequency
                for k in range(BANDS):
                    for e in range(ENERGIES):
                        value = numerator / (squares[k * ENERGIES + e] + squared)
                        pole[k, e * ROWS + r : e * ROWS + r + 16, lanes] = value.astype(jnp.bfloat16)
            return carry

        lax.fori_loop(first, last, one, 0)

    with jax.named_scope("pole"):
        pole_tiles(0, 40)

    core0, core1 = core == 0, core == 1
    core1_first = core1 & (z < 7)

    with jax.named_scope("second"):

        @pl.when(core0)
        def _():
            own0.wait()
            wait(near0.at[pl.ds(0, 7)], first_recv)
            for k in range(BANDS):
                chosen0[k] = near0[owner_x[k] * 2 + owner_core[k], pick[k]]
                for d in range(1, NZ):
                    to = lax.rem(z + d, NZ)

                    @pl.when(to < 7)
                    def _():
                        send(
                            chosen0.at[k, :, pl.ds(lax.rem(to, 7) * LANES, LANES)], far.at[k, z],
                            second_send.at[k], second_recv.at[k], near(x_lo, to, 0),
                        )

        @pl.when(core1_first)
        def _():
            own1.wait()
            wait(near1.at[pl.ds(0, 15)], first_recv)
            for k in range(BANDS):
                chosen1[k] = near1[owner_z[k] * 2 + owner_core[k], pick[k]]
                for d in range(1, XLO):
                    to = lax.rem(x_lo + d, XLO)

                    @pl.when(to < 3)
                    def _():
                        send(
                            chosen1.at[k, :, pl.ds(lax.rem(to, 3) * LANES, LANES)], far.at[k, x_lo],
                            second_send.at[k], second_recv.at[k], near(to, z, 1),
                        )

    with jax.named_scope("pole"):
        pole_tiles(40, TILES)

    core0_tile, core1_tile = core0 & collects, core1 & collects
    lanes0 = pl.ds(pl.multiple_of(x_lo * WIDE0 + lax.rem(z, 7) * LANES, LANES), LANES)
    lanes1 = pl.ds(pl.multiple_of(START1 + lax.rem(z, 7) * WIDE1 + lax.rem(x_lo, 3) * LANES, LANES), LANES)

    with jax.named_scope("spread"):

        @pl.when(core0_tile)
        def _():
            mine = pl.ds(pl.multiple_of(lax.rem(z, 7) * LANES, LANES), LANES)
            for k in range(BANDS):
                wait(far.at[k, pl.ds(0, NZ - 1)], second_recv.at[k])
                total = chosen0[k, :, mine]
                for d in range(NZ):
                    total = jnp.where((owner_z[k] == d) & (z != d), far[k, d], total)
                final[k] = total
                columns[k, :, lanes0] = total
                for d in range(1, NZ):
                    send(final.at[k], columns.at[k, :, lanes0], spread_send.at[k], spread_recv.at[k], along_z(d))

        @pl.when(core1_tile)
        def _():
            mine = pl.ds(pl.multiple_of(lax.rem(x_lo, 3) * LANES, LANES), LANES)
            for k in range(BANDS):
                wait(far.at[k, pl.ds(0, XLO - 1)], second_recv.at[k])
                total = chosen1[k, :, mine]
                for d in range(XLO):
                    total = jnp.where((owner_x[k] == d) & (x_lo != d), far[k, d], total)
                final[k] = total
                columns[k, :, lanes1] = total
                for d in range(1, XLO):
                    send(final.at[k], columns.at[k, :, lanes1], spread_send.at[k], spread_recv.at[k], within_x(d))

        @pl.when(source)
        def _():
            send(final, rows, rows_send.at[0], rows_recv.at[0], (target, 1 - x_hi))

            @pl.when(jnp.logical_not(own_target))
            def _():
                send(final, rows, rows_send.at[1], rows_recv.at[0], (target, x_hi))

            @pl.when(own_target)
            def _():
                for k in range(BANDS):
                    rows[k] = final[k]

    slice0 = pl.ds(pl.multiple_of(x_lo * WIDE0, WIDE0), WIDE0)
    slice1 = pl.ds(pl.multiple_of(START1 + lax.rem(z, 7) * WIDE1, LANES), WIDE1)

    with jax.named_scope("widen"):

        @pl.when(core0)
        def _():
            for k in range(BANDS):
                @pl.when(z < 7)
                def _():
                    wait(far.at[k, pl.ds(0, 6)], spread_recv.at[k])

                @pl.when(z == 7)
                def _():
                    wait(far.at[k, pl.ds(0, 7)], spread_recv.at[k])

                piece = columns.at[k, :, slice0]
                for d in range(1, XLO):
                    send(piece, piece, wide_send.at[k], wide_recv.at[k], within_x(d))

        @pl.when(core1_first)
        def _():
            for k in range(BANDS):
                @pl.when(x_lo < 3)
                def _():
                    wait(far.at[k, pl.ds(0, 2)], spread_recv.at[k])

                @pl.when(x_lo == 3)
                def _():
                    wait(far.at[k, pl.ds(0, 3)], spread_recv.at[k])

                piece = columns.at[k, :, slice1]
                for d in range(1, NZ):
                    send(piece, piece, wide_send.at[k], wide_recv.at[k], along_z(d))

    share[...] = jnp.zeros_like(share)
    whole0 = (slice(None), pl.ds(0, START1))
    whole1 = (slice(None), pl.ds(START1, COLS - START1))

    def forward(k):
        @pl.when(core0)
        def _():
            wait(columns.at[k, :, pl.ds(0, 3 * WIDE0)], wide_recv.at[k])
            half = columns.at[(k, *whole0)]
            send(half, half, pair_send.at[k], pair_recv.at[k], other_core)

        @pl.when(core1)
        def _():
            @pl.when(z < 7)
            def _():
                wait(columns.at[k, :, pl.ds(0, 6 * WIDE1)], wide_recv.at[k])

            @pl.when(z == 7)
            def _():
                wait(columns.at[k, :, pl.ds(0, 7 * WIDE1)], wide_recv.at[k])

            half = columns.at[(k, *whole1)]
            send(half, half, pair_send.at[k], pair_recv.at[k], other_core)

    set0, set1 = pl.ds(0, START1), pl.ds(START1, COLS - START1)

    def dot(k, part):
        return lax.dot_general(
            pole[k, :, part], columns[k, :, part], (((1,), (1,)), ((), ())), preferred_element_type=jnp.float32
        )

    def fold_own(k):
        @pl.when(core0)
        def _():
            folded[k] = dot(k, set0)

        @pl.when(core1)
        def _():
            folded[k] = dot(k, set1)

    def fold_other(k):
        @pl.when(core0)
        def _():
            wait(columns.at[(k, *whole1)], pair_recv.at[k])
            folded[k] += dot(k, set1)

        @pl.when(core1)
        def _():
            wait(columns.at[(k, *whole0)], pair_recv.at[k])
            folded[k] += dot(k, set0)

    with jax.named_scope("forward"):
        forward(0)

    with jax.named_scope("rows"):

        @pl.when(y == 0)
        def _():
            @pl.when(jnp.logical_not(own_target))
            def _():
                wait(rows, rows_recv.at[0])

            for d in range(1, NY):
                send(rows, rows, rows_send.at[2], rows_recv.at[1], along_y(d))

    with jax.named_scope("fold"):
        fold_own(0)

    def advance(k, carry):
        with jax.named_scope("forward"):
            forward(k)
        with jax.named_scope("fold"):
            fold_own(k)
            fold_other(k - 1)
        return carry

    lax.fori_loop(1, BANDS, advance, 0)
    with jax.named_scope("fold"):
        fold_other(BANDS - 1)

    with jax.named_scope("rows"):

        @pl.when(y > 0)
        def _():
            wait(rows, rows_recv.at[1])

    with jax.named_scope("contract"):
        left = jnp.concatenate([rows[k].astype(jnp.float32) for k in range(BANDS)], axis=1)
        right = jnp.concatenate(
            [
                jnp.concatenate([folded[k, e * ROWS : (e + 1) * ROWS] for k in range(BANDS)], axis=0)
                for e in range(ENERGIES)
            ],
            axis=1,
        )
        total = jnp.dot(left, right, precision=lax.Precision.HIGHEST, preferred_element_type=jnp.float32)
        share[:, 0 : ENERGIES * STATES] = total

    packed = jnp.concatenate([share[0:8, 0:64], share[8:16, 0:64]], axis=1)
    for stage, (me, peer) in enumerate(((x, along_x), (y, along_y))):
        totals[stage, me] = packed
        mine = totals.at[stage, me]
        for d in range(1, 8):
            send(mine, mine, sigma_send.at[stage], sigma_recv.at[stage], peer(d))
        with jax.named_scope("sigma"):
            wait(totals.at[stage, pl.ds(0, 7)], sigma_recv.at[stage])
        packed = totals[stage, 0]
        for d in range(1, 8):
            packed = packed + totals[stage, d]
    me = z * 2 + core
    totals_z[me] = packed
    mine = totals_z.at[me]
    for d in range(1, NZ):
        send(mine, mine, sigma_send.at[2], sigma_recv.at[2], along_z(d))
        send(mine, mine, sigma_send.at[2], sigma_recv.at[2], near(x_lo, lax.rem(z + d, NZ), 1 - core))
    send(mine, mine, sigma_send.at[2], sigma_recv.at[2], other_core)
    with jax.named_scope("sigma"):
        wait(totals_z.at[pl.ds(0, 15)], sigma_recv.at[2])
    packed = totals_z[0]
    for d in range(1, 16):
        packed = packed + totals_z[d]

    for e in range(ENERGIES):
        out[e, 0:8] = packed[:, e * STATES : (e + 1) * STATES]
        out[e, 8:16] = packed[:, 64 + e * STATES : 64 + (e + 1) * STATES]

    with jax.named_scope("drain"):
        wait(near0.at[pl.ds(0, 3)], first_send.at[0])

        @pl.when(z < 7)
        def _():
            wait(near1.at[pl.ds(0, 6)], first_send.at[1])

        @pl.when(z == 7)
        def _():
            wait(near1.at[pl.ds(0, 7)], first_send.at[1])

        @pl.when(core0 & (z < 7))
        def _():
            wait(near1.at[0], first_send.at[2])

        @pl.when(core1)
        def _():
            wait(near0.at[0], first_send.at[2])

        for k in range(BANDS):
            @pl.when(core0)
            def _():
                @pl.when(z < 7)
                def _():
                    wait(far.at[k, pl.ds(0, 6)], second_send.at[k])
                    wait(far.at[k, pl.ds(0, 7)], spread_send.at[k])

                @pl.when(z == 7)
                def _():
                    wait(far.at[k, pl.ds(0, 7)], second_send.at[k])

                wait(columns.at[k, :, pl.ds(0, 3 * WIDE0)], wide_send.at[k])
                wait(columns.at[(k, *whole0)], pair_send.at[k])

            @pl.when(core1)
            def _():
                @pl.when(z < 7)
                def _():
                    @pl.when(x_lo < 3)
                    def _():
                        wait(far.at[k, pl.ds(0, 2)], second_send.at[k])
                        wait(far.at[k, pl.ds(0, 3)], spread_send.at[k])

                    @pl.when(x_lo == 3)
                    def _():
                        wait(far.at[k, pl.ds(0, 3)], second_send.at[k])

                    wait(columns.at[k, :, pl.ds(0, 7 * WIDE1)], wide_send.at[k])

                wait(columns.at[(k, *whole1)], pair_send.at[k])

        @pl.when(source)
        def _():
            wait(rows, rows_send.at[0])

            @pl.when(jnp.logical_not(own_target))
            def _():
                wait(rows, rows_send.at[1])

        @pl.when(y == 0)
        def _():
            wait(far.at[:, pl.ds(0, 7)], rows_send.at[2])

        for stage in range(2):
            wait(totals.at[stage, pl.ds(0, 7)], sigma_send.at[stage])
        wait(totals_z.at[pl.ds(0, 15)], sigma_send.at[2])


def shards(matel, pole_amp, pole_freq, band_energy, energies, owner, slot):
    bf16, f32 = jnp.bfloat16, jnp.float32
    dma = pltpu.SemaphoreType.DMA
    return pl.pallas_call(
        kernel,
        out_shape=jax.ShapeDtypeStruct((ENERGIES, STATES, STATES), f32),
        in_specs=[pl.BlockSpec(memory_space=pl.ANY)] * 7,
        out_specs=pl.BlockSpec(memory_space=pltpu.VMEM),
        scratch_shapes=[
            pltpu.SMEM(owner.shape, owner.dtype),
            pltpu.SMEM(slot.shape, slot.dtype),
            pltpu.SMEM(band_energy.shape, f32),
            pltpu.SMEM(energies.shape, f32),
            pltpu.VMEM((ROWS, COLS), bf16),
            pltpu.VMEM((ROWS, COLS), bf16),
            pltpu.VMEM((2 * XLO, 2, STATES, WIDE0), bf16),
            pltpu.VMEM((2 * NZ, 2, STATES, WIDE1), bf16),
            pltpu.VMEM((BANDS, STATES, WIDE0), bf16),
            pltpu.VMEM((BANDS, STATES, WIDE1), bf16),
            pltpu.VMEM((BANDS, NZ, STATES, LANES), bf16),
            pltpu.VMEM((BANDS, STATES, LANES), bf16),
            pltpu.VMEM((BANDS, STATES, COLS), bf16),
            pltpu.VMEM((BANDS, ENERGIES * ROWS, COLS), bf16),
            pltpu.VMEM((BANDS, STATES, LANES), bf16),
            pltpu.VMEM((BANDS, ENERGIES * ROWS, STATES), f32),
            pltpu.VMEM((STATES, LANES), f32),
            pltpu.VMEM((2, 8, 8, LANES), f32),
            pltpu.VMEM((16, 8, LANES), f32),
            dma((3,)), dma((4,)), dma((3,)), dma,
        ] + [dma((BANDS,))] * 8 + [dma((3,)), dma((2,)), dma((3,)), dma((3,))],
        compiler_params=pltpu.CompilerParams(
            collective_id=0, has_side_effects=True, vmem_limit_bytes=60 * 1024 * 1024
        ),
    )(owner, slot, band_energy, energies, matel, pole_amp, pole_freq)


def solution(mesh):
    return jax.shard_map(
        shards,
        mesh=mesh,
        in_specs=(P("ga", None, "gp"), P("ga", "gp"), P("ga", "gp"), P(), P(), P(), P()),
        out_specs=P(),
        check_vma=False,
    )
```

```python
import jax
import jax.numpy as jnp
from jax import lax
from jax.experimental import pallas as pl
from jax.experimental.pallas import tpu as pltpu
from jax.sharding import PartitionSpec as P

MESH = pl.DeviceIdType.MESH
NX, NY, NZ = 8, 8, 8
XLO = 4
LANES = 128
BANDS = 5
ENERGIES = 3
STATES = 16
ROWS = 128
TILES = 49
WIDE0, WIDE1 = 7 * LANES, 3 * LANES
START1 = 28 * LANES
COLS = TILES * LANES


def kernel(
    owner_in, slot_in, band_energy_in, energies_in, matel, amp, freq, out,
    owner, slot, band_energy, energies,
    amp_v, freq_v, near0, near1, chosen0, chosen1, far, final, columns, pole, rows, folded, share, totals, totals_z,
    load_sem, small_sem, first_send, first_recv, second_send, second_recv, spread_send, spread_recv,
    wide_send, wide_recv, pair_send, pair_recv, rows_send, rows_recv, sigma_send, sigma_recv,
):
    ga, gp = lax.axis_index("ga"), lax.axis_index("gp")
    x_lo, z, core = lax.div(ga, 16), lax.rem(lax.div(ga, 2), NZ), lax.rem(ga, 2)
    y, x_hi = lax.div(gp, 2), lax.rem(gp, 2)
    x = x_hi * XLO + x_lo

    def device(x_at, y_at, z_at, core_at):
        return (
            lax.rem(x_at, XLO) * 16 + z_at * 2 + core_at,
            y_at * 2 + lax.div(x_at, XLO),
        )

    def near(x_lo_at, z_at, core_at):
        return (x_lo_at * 16 + z_at * 2 + core_at, gp)

    def along_x(d):
        return device(lax.rem(x + d, NX), y, z, core)

    def along_y(d):
        return device(x, lax.rem(y + d, NY), z, core)

    def along_z(d):
        return near(x_lo, lax.rem(z + d, NZ), core)

    def within_x(d):
        return near(lax.rem(x_lo + d, XLO), z, core)

    other_core = near(x_lo, z, 1 - core)

    def send(src, dst, send_sem, recv_sem, to):
        pltpu.make_async_remote_copy(
            src_ref=src, dst_ref=dst, send_sem=send_sem, recv_sem=recv_sem,
            device_id=to, device_id_type=MESH,
        ).start()

    def wait(ref, sem):
        pltpu.make_async_copy(ref, ref, sem).wait()

    small = [
        pltpu.make_async_copy(src, dst, small_sem.at[i])
        for i, (src, dst) in enumerate(
            ((owner_in, owner), (slot_in, slot), (band_energy_in, band_energy), (energies_in, energies))
        )
    ]
    def each(first, last, body):
        def step(i, carry):
            body(i)
            return carry

        lax.fori_loop(first, last, step, 0)

    load_amp = pltpu.make_async_copy(amp, amp_v, load_sem.at[1])
    load_freq = pltpu.make_async_copy(freq, freq_v, load_sem.at[2])

    tile = jnp.where(core == 0, x_lo * 7 + z, 28 + z * 3 + x_lo)
    collects = (z < 7) & ((core == 0) | (x_lo < 3))
    source = (y == 0) & collects & ((x_hi == 0) | (tile < 15))
    target = tile + jnp.where(x_hi == 0, 0, TILES)
    own_target = source & (target == ga)
    wanted = jnp.where(ga < TILES, ga, ga - TILES)
    wanted_hi = jnp.where(ga < TILES, 0, 1)
    second_set = jnp.maximum(wanted - 28, 0)
    collector = jnp.where(
        wanted < 28,
        lax.div(wanted, 7) * 16 + lax.rem(wanted, 7) * 2,
        lax.rem(second_set, 3) * 16 + lax.div(second_set, 3) * 2 + 1,
    )
    own_collector = (collector == ga) & (x_hi == wanted_hi)

    barrier = pltpu.get_barrier_semaphore()

    def signal(to):
        pl.semaphore_signal(barrier, inc=1, device_id=to, device_id_type=MESH)

    signal(other_core)

    def greet(d):
        signal(along_z(d))
        signal(near(x_lo, lax.rem(z + d, NZ), 1 - core))
        signal(along_x(d))
        signal(along_y(d))

    each(1, 8, greet)
    each(1, XLO, lambda d: signal(near(lax.rem(x_lo + d, XLO), z, 1 - core)))

    @pl.when((y == 0) & jnp.logical_not(own_collector))
    def _():
        signal((collector, wanted_hi))

    for copy in small:
        copy.start()
    load_amp.start()
    load_freq.start()
    extra = jnp.where(source, 2, 0) - jnp.where(own_target, 1, 0)
    with jax.named_scope("barrier"):
        pl.semaphore_wait(barrier, 32 + extra)

    own0 = pltpu.make_async_copy(
        matel.at[:, :, pl.ds(x_lo * WIDE0, WIDE0)], near0.at[x_lo * 2], load_sem.at[0]
    )
    own1 = pltpu.make_async_copy(
        matel.at[:, :, pl.ds(START1 + lax.rem(z, 7) * WIDE1, WIDE1)], near1.at[z * 2 + 1], load_sem.at[0]
    )
    def first_x(d):
        to = lax.rem(x_lo + d, XLO)
        send(
            matel.at[:, :, pl.ds(pl.multiple_of(to * WIDE0, LANES), WIDE0)], near0.at[x_lo * 2 + core],
            first_send.at[0], first_recv, near(to, z, 0),
        )

    def first_z(d):
        to = lax.rem(z + d, NZ)

        @pl.when(to < 7)
        def _():
            start = pl.multiple_of(START1 + lax.rem(to, 7) * WIDE1, LANES)
            send(
                matel.at[:, :, pl.ds(start, WIDE1)], near1.at[z * 2 + core],
                first_send.at[1], first_recv, near(x_lo, to, 1),
            )

    each(1, XLO, first_x)
    each(1, NZ, first_z)

    @pl.when(core == 0)
    def _():
        own0.start()

        @pl.when(z < 7)
        def _():
            send(
                matel.at[:, :, pl.ds(START1 + lax.rem(z, 7) * WIDE1, WIDE1)], near1.at[z * 2],
                first_send.at[2], first_recv, other_core,
            )

    @pl.when(core == 1)
    def _():
        send(
            matel.at[:, :, pl.ds(x_lo * WIDE0, WIDE0)], near0.at[x_lo * 2 + 1],
            first_send.at[2], first_recv, other_core,
        )

        @pl.when(z < 7)
        def _():
            own1.start()

    for copy in small:
        copy.wait()

    def owner_x(k):
        return lax.div(owner[k], 16)

    def owner_z(k):
        return lax.rem(lax.div(owner[k], 2), NZ)

    def owner_core(k):
        return lax.rem(owner[k], 2)

    squares = []
    for k in range(BANDS):
        level = band_energy[owner[k] * 2 + slot[k]]
        for e in range(ENERGIES):
            detuning = energies[e] - level
            squares.append(detuning * detuning)

    load_amp.wait()
    load_freq.wait()

    def pole_tiles(first, last):
        def one(at, carry):
            lanes = pl.ds(pl.multiple_of(at * LANES, LANES), LANES)
            for r in range(0, ROWS, 16):
                amplitude = amp_v[r : r + 16, lanes].astype(jnp.float32)
                frequency = freq_v[r : r + 16, lanes].astype(jnp.float32)
                numerator = amplitude * frequency
                squared = frequency * frequency
                for k in range(BANDS):
                    for e in range(ENERGIES):
                        value = numerator / (squares[k * ENERGIES + e] + squared)
                        pole[k, e * ROWS + r : e * ROWS + r + 16, lanes] = value.astype(jnp.bfloat16)
            return carry

        lax.fori_loop(first, last, one, 0)

    with jax.named_scope("pole"):
        pole_tiles(0, 40)

    core0, core1 = core == 0, core == 1
    core1_first = core1 & (z < 7)

    with jax.named_scope("second"):

        @pl.when(core0)
        def _():
            own0.wait()
            wait(near0.at[pl.ds(0, 7)], first_recv)

            def band(k):
                chosen0[k] = near0[owner_x(k) * 2 + owner_core(k), slot[k]]

                def one(d):
                    to = lax.rem(z + d, NZ)

                    @pl.when(to < 7)
                    def _():
                        lanes = pl.ds(pl.multiple_of(lax.rem(to, 7) * LANES, LANES), LANES)
                        send(
                            chosen0.at[k, :, lanes], far.at[k, z],
                            second_send.at[k], second_recv.at[k], near(x_lo, to, 0),
                        )

                each(1, NZ, one)

            each(0, BANDS, band)

        @pl.when(core1_first)
        def _():
            own1.wait()
            wait(near1.at[pl.ds(0, 15)], first_recv)

            def band(k):
                chosen1[k] = near1[owner_z(k) * 2 + owner_core(k), slot[k]]

                def one(d):
                    to = lax.rem(x_lo + d, XLO)

                    @pl.when(to < 3)
                    def _():
                        lanes = pl.ds(pl.multiple_of(lax.rem(to, 3) * LANES, LANES), LANES)
                        send(
                            chosen1.at[k, :, lanes], far.at[k, x_lo],
                            second_send.at[k], second_recv.at[k], near(to, z, 1),
                        )

                each(1, XLO, one)

            each(0, BANDS, band)

    with jax.named_scope("pole"):
        pole_tiles(40, TILES)

    core0_tile, core1_tile = core0 & collects, core1 & collects
    lanes0 = pl.ds(pl.multiple_of(x_lo * WIDE0 + lax.rem(z, 7) * LANES, LANES), LANES)
    lanes1 = pl.ds(pl.multiple_of(START1 + lax.rem(z, 7) * WIDE1 + lax.rem(x_lo, 3) * LANES, LANES), LANES)

    with jax.named_scope("spread"):

        @pl.when(core0_tile)
        def _():
            mine = pl.ds(pl.multiple_of(lax.rem(z, 7) * LANES, LANES), LANES)

            def band(k):
                wait(far.at[k, pl.ds(0, NZ - 1)], second_recv.at[k])
                total = chosen0[k, :, mine]
                for d in range(NZ):
                    total = jnp.where((owner_z(k) == d) & (z != d), far[k, d], total)
                final[k] = total
                columns[k, :, lanes0] = total
                each(1, NZ, lambda d: send(
                    final.at[k], columns.at[k, :, lanes0], spread_send.at[k], spread_recv.at[k], along_z(d)))

            each(0, BANDS, band)

        @pl.when(core1_tile)
        def _():
            mine = pl.ds(pl.multiple_of(lax.rem(x_lo, 3) * LANES, LANES), LANES)

            def band(k):
                wait(far.at[k, pl.ds(0, XLO - 1)], second_recv.at[k])
                total = chosen1[k, :, mine]
                for d in range(XLO):
                    total = jnp.where((owner_x(k) == d) & (x_lo != d), far[k, d], total)
                final[k] = total
                columns[k, :, lanes1] = total
                each(1, XLO, lambda d: send(
                    final.at[k], columns.at[k, :, lanes1], spread_send.at[k], spread_recv.at[k], within_x(d)))

            each(0, BANDS, band)

        @pl.when(source)
        def _():
            send(final, rows, rows_send.at[0], rows_recv.at[0], (target, 1 - x_hi))

            @pl.when(jnp.logical_not(own_target))
            def _():
                send(final, rows, rows_send.at[1], rows_recv.at[0], (target, x_hi))

            @pl.when(own_target)
            def _():
                for k in range(BANDS):
                    rows[k] = final[k]

    slice0 = pl.ds(pl.multiple_of(x_lo * WIDE0, WIDE0), WIDE0)
    slice1 = pl.ds(pl.multiple_of(START1 + lax.rem(z, 7) * WIDE1, LANES), WIDE1)

    with jax.named_scope("widen"):

        @pl.when(core0)
        def _():
            def band(k):
                @pl.when(z < 7)
                def _():
                    wait(far.at[k, pl.ds(0, 6)], spread_recv.at[k])

                @pl.when(z == 7)
                def _():
                    wait(far.at[k, pl.ds(0, 7)], spread_recv.at[k])

                piece = columns.at[k, :, slice0]
                each(1, XLO, lambda d: send(piece, piece, wide_send.at[k], wide_recv.at[k], within_x(d)))

            each(0, BANDS, band)

        @pl.when(core1_first)
        def _():
            def band(k):
                @pl.when(x_lo < 3)
                def _():
                    wait(far.at[k, pl.ds(0, 2)], spread_recv.at[k])

                @pl.when(x_lo == 3)
                def _():
                    wait(far.at[k, pl.ds(0, 3)], spread_recv.at[k])

                piece = columns.at[k, :, slice1]
                each(1, NZ, lambda d: send(piece, piece, wide_send.at[k], wide_recv.at[k], along_z(d)))

            each(0, BANDS, band)

    share[...] = jnp.zeros_like(share)
    whole0 = (slice(None), pl.ds(0, START1))
    whole1 = (slice(None), pl.ds(START1, COLS - START1))

    def forward(k):
        @pl.when(core0)
        def _():
            wait(columns.at[k, :, pl.ds(0, 3 * WIDE0)], wide_recv.at[k])
            half = columns.at[(k, *whole0)]
            send(half, half, pair_send.at[k], pair_recv.at[k], other_core)

        @pl.when(core1)
        def _():
            @pl.when(z < 7)
            def _():
                wait(columns.at[k, :, pl.ds(0, 6 * WIDE1)], wide_recv.at[k])

            @pl.when(z == 7)
            def _():
                wait(columns.at[k, :, pl.ds(0, 7 * WIDE1)], wide_recv.at[k])

            half = columns.at[(k, *whole1)]
            send(half, half, pair_send.at[k], pair_recv.at[k], other_core)

    set0, set1 = pl.ds(0, START1), pl.ds(START1, COLS - START1)

    def dot(k, part):
        return lax.dot_general(
            pole[k, :, part], columns[k, :, part], (((1,), (1,)), ((), ())), preferred_element_type=jnp.float32
        )

    def fold_own(k):
        @pl.when(core0)
        def _():
            folded[k] = dot(k, set0)

        @pl.when(core1)
        def _():
            folded[k] = dot(k, set1)

    def fold_other(k):
        @pl.when(core0)
        def _():
            wait(columns.at[(k, *whole1)], pair_recv.at[k])
            folded[k] += dot(k, set1)

        @pl.when(core1)
        def _():
            wait(columns.at[(k, *whole0)], pair_recv.at[k])
            folded[k] += dot(k, set0)

    with jax.named_scope("forward"):
        forward(0)

    with jax.named_scope("rows"):

        @pl.when(y == 0)
        def _():
            @pl.when(jnp.logical_not(own_target))
            def _():
                wait(rows, rows_recv.at[0])

            each(1, NY, lambda d: send(rows, rows, rows_send.at[2], rows_recv.at[1], along_y(d)))

    with jax.named_scope("fold"):
        fold_own(0)

    def advance(k, carry):
        with jax.named_scope("forward"):
            forward(k)
        with jax.named_scope("fold"):
            fold_own(k)
            fold_other(k - 1)
        return carry

    lax.fori_loop(1, BANDS, advance, 0)
    with jax.named_scope("fold"):
        fold_other(BANDS - 1)

    with jax.named_scope("rows"):

        @pl.when(y > 0)
        def _():
            wait(rows, rows_recv.at[1])

    with jax.named_scope("contract"):
        left = jnp.concatenate([rows[k].astype(jnp.float32) for k in range(BANDS)], axis=1)
        right = jnp.concatenate(
            [
                jnp.concatenate([folded[k, e * ROWS : (e + 1) * ROWS] for k in range(BANDS)], axis=0)
                for e in range(ENERGIES)
            ],
            axis=1,
        )
        total = jnp.dot(left, right, precision=lax.Precision.HIGHEST, preferred_element_type=jnp.float32)
        share[:, 0 : ENERGIES * STATES] = total

    packed = jnp.concatenate([share[0:8, 0:64], share[8:16, 0:64]], axis=1)
    for stage, (me, peer) in enumerate(((x, along_x), (y, along_y))):
        totals[stage, me] = packed
        mine = totals.at[stage, me]
        each(1, 8, lambda d: send(mine, mine, sigma_send.at[stage], sigma_recv.at[stage], peer(d)))
        with jax.named_scope("sigma"):
            wait(totals.at[stage, pl.ds(0, 7)], sigma_recv.at[stage])
        packed = totals[stage, 0]
        for d in range(1, 8):
            packed = packed + totals[stage, d]
    me = z * 2 + core
    totals_z[me] = packed
    mine = totals_z.at[me]

    def last(d):
        send(mine, mine, sigma_send.at[2], sigma_recv.at[2], along_z(d))
        send(mine, mine, sigma_send.at[2], sigma_recv.at[2], near(x_lo, lax.rem(z + d, NZ), 1 - core))

    each(1, NZ, last)
    send(mine, mine, sigma_send.at[2], sigma_recv.at[2], other_core)
    with jax.named_scope("sigma"):
        wait(totals_z.at[pl.ds(0, 15)], sigma_recv.at[2])
    packed = totals_z[0]
    for d in range(1, 16):
        packed = packed + totals_z[d]

    for e in range(ENERGIES):
        out[e, 0:8] = packed[:, e * STATES : (e + 1) * STATES]
        out[e, 8:16] = packed[:, 64 + e * STATES : 64 + (e + 1) * STATES]

    with jax.named_scope("drain"):
        wait(near0.at[pl.ds(0, 3)], first_send.at[0])

        @pl.when(z < 7)
        def _():
            wait(near1.at[pl.ds(0, 6)], first_send.at[1])

        @pl.when(z == 7)
        def _():
            wait(near1.at[pl.ds(0, 7)], first_send.at[1])

        @pl.when(core0 & (z < 7))
        def _():
            wait(near1.at[0], first_send.at[2])

        @pl.when(core1)
        def _():
            wait(near0.at[0], first_send.at[2])

        def drain(k):
            @pl.when(core0)
            def _():
                @pl.when(z < 7)
                def _():
                    wait(far.at[k, pl.ds(0, 6)], second_send.at[k])
                    wait(far.at[k, pl.ds(0, 7)], spread_send.at[k])

                @pl.when(z == 7)
                def _():
                    wait(far.at[k, pl.ds(0, 7)], second_send.at[k])

                wait(columns.at[k, :, pl.ds(0, 3 * WIDE0)], wide_send.at[k])
                wait(columns.at[(k, *whole0)], pair_send.at[k])

            @pl.when(core1)
            def _():
                @pl.when(z < 7)
                def _():
                    @pl.when(x_lo < 3)
                    def _():
                        wait(far.at[k, pl.ds(0, 2)], second_send.at[k])
                        wait(far.at[k, pl.ds(0, 3)], spread_send.at[k])

                    @pl.when(x_lo == 3)
                    def _():
                        wait(far.at[k, pl.ds(0, 3)], second_send.at[k])

                    wait(columns.at[k, :, pl.ds(0, 7 * WIDE1)], wide_send.at[k])

                wait(columns.at[(k, *whole1)], pair_send.at[k])

        each(0, BANDS, drain)

        @pl.when(source)
        def _():
            wait(rows, rows_send.at[0])

            @pl.when(jnp.logical_not(own_target))
            def _():
                wait(rows, rows_send.at[1])

        @pl.when(y == 0)
        def _():
            wait(far.at[:, pl.ds(0, 7)], rows_send.at[2])

        for stage in range(2):
            wait(totals.at[stage, pl.ds(0, 7)], sigma_send.at[stage])
        wait(totals_z.at[pl.ds(0, 15)], sigma_send.at[2])


def shards(matel, pole_amp, pole_freq, band_energy, energies, owner, slot):
    bf16, f32 = jnp.bfloat16, jnp.float32
    dma = pltpu.SemaphoreType.DMA
    return pl.pallas_call(
        kernel,
        out_shape=jax.ShapeDtypeStruct((ENERGIES, STATES, STATES), f32),
        in_specs=[pl.BlockSpec(memory_space=pl.ANY)] * 7,
        out_specs=pl.BlockSpec(memory_space=pltpu.VMEM),
        scratch_shapes=[
            pltpu.SMEM(owner.shape, owner.dtype),
            pltpu.SMEM(slot.shape, slot.dtype),
            pltpu.SMEM(band_energy.shape, f32),
            pltpu.SMEM(energies.shape, f32),
            pltpu.VMEM((ROWS, COLS), bf16),
            pltpu.VMEM((ROWS, COLS), bf16),
            pltpu.VMEM((2 * XLO, 2, STATES, WIDE0), bf16),
            pltpu.VMEM((2 * NZ, 2, STATES, WIDE1), bf16),
            pltpu.VMEM((BANDS, STATES, WIDE0), bf16),
            pltpu.VMEM((BANDS, STATES, WIDE1), bf16),
            pltpu.VMEM((BANDS, NZ, STATES, LANES), bf16),
            pltpu.VMEM((BANDS, STATES, LANES), bf16),
            pltpu.VMEM((BANDS, STATES, COLS), bf16),
            pltpu.VMEM((BANDS, ENERGIES * ROWS, COLS), bf16),
            pltpu.VMEM((BANDS, STATES, LANES), bf16),
            pltpu.VMEM((BANDS, ENERGIES * ROWS, STATES), f32),
            pltpu.VMEM((STATES, LANES), f32),
            pltpu.VMEM((2, 8, 8, LANES), f32),
            pltpu.VMEM((16, 8, LANES), f32),
            dma((3,)), dma((4,)), dma((3,)), dma,
        ] + [dma((BANDS,))] * 8 + [dma((3,)), dma((2,)), dma((3,)), dma((3,))],
        compiler_params=pltpu.CompilerParams(
            collective_id=0, has_side_effects=True, vmem_limit_bytes=60 * 1024 * 1024
        ),
    )(owner, slot, band_energy, energies, matel, pole_amp, pole_freq)


def solution(mesh):
    return jax.shard_map(
        shards,
        mesh=mesh,
        in_specs=(P("ga", None, "gp"), P("ga", "gp"), P("ga", "gp"), P(), P(), P(), P()),
        out_specs=P(),
        check_vma=False,
    )
```
